32 devices in a mesh: groups: 2 (over y), wide: 4 (over z), tail: 2 (over x), sub: 2 (over core).
Axes of the slice: x: 2, y: 2, z: 4, core: 2. Of those that a mesh axis runs over, the one named last changes fastest.
Arguments:
- head_embed: float32 [512, 512], P(('groups', 'wide')), parts along dimension 0, may hold values from -2.1 to 2.1
- tail_embed: float32 [512, 512], P(('groups', 'tail'), 'sub'), parts along dimension 0, may hold values from -2.1 to 2.1
- core_mats: float32 [8, 512, 512], P(('groups', 'wide'), None, 'sub'), parts along dimension 0, may hold values from -0.25 to 0.25
- labels: int32 [512, 8, 256], P(('groups', 'wide'), None, 'tail'), parts along dimension 0, may hold values 0 or 1
- core_lists: int32 [4, 8], P(('groups', 'tail')), parts along dimension 0, may hold values from 0 to 3, as said below
Outputs:
- grad_head: float32 [512, 512], P(('groups', 'wide', 'tail', 'sub')), parts along dimension 0
- grad_tail: float32 [4, 128, 512], P(('groups', 'tail'), 'wide', 'sub'), parts along dimension 0
- grad_cores: float32 [8, 512, 512], P(('groups', 'tail'), 'wide', 'sub'), parts along dimension 0
The draws below stay inside these ranges and needn't reach their ends.
There are 2 independent parts, one for each index of `groups`. The reference program is written for one: setup_inputs(seed, part) draws one part's arguments, and reference() takes and returns one part's arrays. A program takes and returns all parts, laid end to end along the dimension named above; each array names one. Nothing has to cross between parts.
Inputs may be any that keep to these rules, and one draw needn't show every extreme that they name: `core_lists`: every one of the 4 core ids stands somewhere in the lists; ids may repeat.
All inputs are finite; a program needn't handle non-finite values. No bound on the sum of `labels` on one device may be relied on, other than what follows from the above.
Results may differ from the reference program's by a relative error of at most 0.0001.
Values sent between devices are 32-bit elements; how exact they have to be, the bound alone decides.
A program may use at most 64 MiB of HBM per device.

```python
import math
import jax
import jax.numpy as jnp
from jax import lax

D = 512
LIST = 8
T_DEV = 128
NREL = 4
HEADS = 256
TAILS = 256
COLUMNS = 2


def draw_core_lists(key, part):
    first_key, second_key, third_key = jax.random.split(key, 3)
    covering = jax.random.permutation(first_key, NREL).astype(jnp.int32)
    remainder = jax.random.randint(second_key, (COLUMNS * LIST - NREL,), 0, NREL).astype(jnp.int32)
    flattened = jnp.concatenate([covering, remainder])
    shuffle_order = jax.random.permutation(third_key, COLUMNS * LIST)
    return flattened[shuffle_order].reshape(COLUMNS, LIST)


def set_ends(values, key, least, high):
    index_at = [jax.random.randint(jax.random.fold_in(key, axis), (), 0, length) for axis, length in enumerate(values.shape)]
    main_axis = values.shape.index(max(values.shape))
    beside = index_at[:main_axis] + [(index_at[main_axis] + 1) % values.shape[main_axis]] + index_at[main_axis + 1:]
    return values.at[tuple(index_at)].set(least).at[tuple(beside)].set(high)


def levels(rng, dims, cuts, least, top_value):
    gain, own = 1.0, jax.random.fold_in(rng, 6)
    for dim, parts in cuts:
        draws = jnp.exp(jax.random.uniform(jax.random.fold_in(own, dim), (parts,), jnp.float32, least / len(cuts), top_value / len(cuts)))
        gain = gain * jnp.repeat(draws, dims[dim] // parts).reshape([-1 if axis == dim else 1 for axis in range(len(dims))])
    return gain


def centred(own_key, extent, width, reach, shards=(), dtype=jnp.bfloat16):
    entries = jax.random.normal(own_key, extent, jnp.float32) * width
    if len(shards) > 0:
        entries = levels(own_key, extent, shards, -0.22, 0.18) * entries
    return jnp.clip(entries, min=-reach, max=reach).astype(dtype)


def setup_inputs(seed: int = 0, part: int = 0) -> dict:
    key_of = jax.random.split(jax.random.key(seed), 6)
    part_keys = jax.random.split(jax.random.fold_in(key_of[5], part), 6)
    return {
        "head_embed": centred(part_keys[0], (HEADS, D), 0.35, 2.1, ((0, 4),), jnp.float32),
        "tail_embed": centred(part_keys[1], (TAILS, D), 0.35, 2.1, ((0, 2), (1, 2)), jnp.float32),
        "core_mats": centred(part_keys[2], (NREL, D, D), D ** -0.5, 0.25, ((0, 4), (2, 2)), jnp.float32),
        "labels": set_ends((jax.random.randint(part_keys[3], (HEADS, LIST, TAILS), 0, 2) < 1).astype(jnp.int32), jax.random.fold_in(part_keys[3], 1), 0, 1),
        "core_lists": draw_core_lists(jax.random.fold_in(jax.random.fold_in(key_of[5], part), 71), part),
    }


def reference(head_embed, tail_embed, core_mats, labels, core_lists):
    highest = lax.Precision.HIGHEST
    grad_head = jnp.zeros((HEADS, D), jnp.float32)
    grad_cores = jnp.zeros((NREL, D, D), jnp.float32)
    tail_blocks = []
    for column in range(COLUMNS):
        tail_tile = tail_embed[column * T_DEV:(column + 1) * T_DEV]
        tail_total = jnp.zeros((T_DEV, D), jnp.float32)
        for slot_index in range(LIST):
            relation = core_lists[column, slot_index].astype(jnp.int32)
            matrix = lax.dynamic_index_in_dim(core_mats, relation, 0, keepdims=False)
            projected = jnp.dot(head_embed, matrix, precision=highest, preferred_element_type=jnp.float32)
            score_tile = jnp.dot(projected, tail_tile.T, precision=highest, preferred_element_type=jnp.float32)
            label_tile = labels[:, slot_index, column * T_DEV:(column + 1) * T_DEV].astype(jnp.float32)
            residual = jax.nn.sigmoid(score_tile) - label_tile
            weighted = jnp.dot(residual, tail_tile, precision=highest, preferred_element_type=jnp.float32)
            grad_head = grad_head + jnp.dot(weighted, matrix.T, precision=highest, preferred_element_type=jnp.float32)
            tail_total = tail_total + jnp.dot(residual.T, projected, precision=highest, preferred_element_type=jnp.float32)
            core_term = jnp.dot(head_embed.T, weighted, precision=highest, preferred_element_type=jnp.float32)
            grad_cores = grad_cores.at[relation].add(core_term)
        tail_blocks.append(tail_total)
    grad_tail = jnp.stack(tail_blocks)
    return (grad_head * (1.0 / math.sqrt(LIST * TAILS)), grad_tail * (1.0 / math.sqrt(LIST * HEADS)), grad_cores * (1.0 / math.sqrt(HEADS * T_DEV)))
```

```python
import functools
import math

import jax
import jax.numpy as jnp
from jax import lax
from jax.experimental import pallas as pl
from jax.experimental.pallas import tpu as pltpu
from jax.sharding import PartitionSpec as P

MESH = pl.DeviceIdType.MESH
F32 = jnp.float32
BF16 = jnp.bfloat16
NN = (((1,), (0,)), ((), ()))
NT = (((1,), (1,)), ((), ()))


def split(value):
    high = value.astype(BF16)
    return high, (value - high.astype(F32)).astype(BF16)


def dot3(a, b, dims):
    one = lambda x, y: lax.dot_general(x, y, dims, preferred_element_type=F32)
    return one(a[0], b[0]) + (one(a[0], b[1]) + one(a[1], b[0]))


def kernel(
    wides, tails, per_tail, scales,
    lists, head, tail, core, labels,
    head_out, tail_out, core_out,
    heads, count_out, count_in, core_far, tail_far, tail_x, rho_z, rho_x,
    tp_out, tp_in, tp_sum, tp_z, hg, hg_x, hg_sum, hg_z, g_out, g_in,
    sib_send, sib_recv, z_send, z_recv, x_send, x_recv,
):
    w, t, s = lax.axis_index("wide"), lax.axis_index("tail"), lax.axis_index("sub")
    sibling = {"sub": 1 - s}
    z_peers = [lax.rem(w + k, wides) for k in range(1, wides)]
    x_peers = [lax.rem(t + k, tails) for k in range(1, tails)]
    part = heads.shape[2]
    width = heads.shape[3]
    tail_rows, half = tail.shape
    slots = labels.shape[1]
    row_count = tails * wides * part

    def copy(src, dst, send, recv, device):
        return pltpu.make_async_remote_copy(
            src_ref=src, dst_ref=dst, send_sem=send, recv_sem=recv,
            device_id=device, device_id_type=MESH,
        )

    sent = []

    def put(src, dst, send, recv, device):
        job = copy(src, dst, send, recv, device)
        job.start()
        sent.append(job)

    def arrived(dst, send, recv, device):
        copy(dst, dst, send, recv, device).wait_recv()

    def put_sub(kind, src, dst):
        put(src, dst, sib_send.at[kind], sib_recv.at[kind], sibling)

    def take_sub(kind, dst):
        arrived(dst, sib_send.at[kind], sib_recv.at[kind], sibling)

    def put_z(kind, k, src, dst):
        put(src, dst, z_send.at[kind, k], z_recv.at[kind, w], {"wide": z_peers[k]})

    def take_z(kind, p, dst):
        arrived(dst, z_send.at[kind, 0], z_recv.at[kind, p], {"wide": z_peers[0]})

    def put_x(kind, k, src, dst):
        put(src, dst, x_send.at[kind, k], x_recv.at[kind, t], {"tail": x_peers[k]})

    def take_x(kind, p, dst):
        arrived(dst, x_send.at[kind, 0], x_recv.at[kind, p], {"tail": x_peers[0]})

    barrier = pltpu.get_barrier_semaphore()
    partners = [sibling] + [{"wide": p} for p in z_peers] + [{"tail": p} for p in x_peers]
    for device in partners:
        pl.semaphore_signal(barrier, inc=1, device_id=device, device_id_type=MESH)
    for tau in range(tails):
        start = pl.multiple_of((tau * 2 + s) * part, part)
        heads[tau, w] = head[pl.ds(start, part), :]
    pl.semaphore_wait(barrier, len(partners))

    for k in reversed(range(len(z_peers))):
        put_z(0, k, heads.at[:, w], heads.at[:, w])
    put_sub(0, core.at[0], core_far)
    put_sub(1, tail, tail_far)
    for k in range(len(x_peers)):
        put_x(0, k, tail, tail_x.at[t, 0])

    shape = (wides, part, part * slots)
    lane = lax.broadcasted_iota(jnp.int32, shape, 2)
    offset = lane - slots * lax.broadcasted_iota(jnp.int32, shape, 1)
    listed = jnp.full(shape, -1, jnp.int32)
    for j in range(slots):
        listed = jnp.where(offset == j, lists[0, j], listed)
    picks = jnp.where(listed == lax.broadcasted_iota(jnp.int32, shape, 0), 1.0, 0.0)
    picks = picks.reshape(wides * part, part * slots).astype(BF16)
    for tau in range(tails):
        start = (tau * 2 + s) * part
        block = labels[pl.ds(start, part)].reshape(part * slots, tail_rows)
        counts = lax.dot_general(
            picks, block.astype(F32).astype(BF16), NN, preferred_element_type=F32
        )
        count_out[:, tau] = counts.reshape(wides, part, tail_rows)
    for k, p in enumerate(z_peers):
        put_z(1, k, count_out.at[p], count_in.at[:, w])
    count_in[:, w] = count_out[w]
    uses = jnp.float32(0.0)
    for j in range(slots):
        uses = uses + (lists[0, j] == w).astype(F32)

    core_near = split(core[0])
    tail_near = split(tail[...])
    take_sub(0, core_far)
    core_away = split(core_far[...])
    take_sub(1, tail_far)
    tail_away = split(tail_far[...])
    for p in z_peers:
        take_z(0, p, heads.at[:, p])
    all_heads = split(heads[...].reshape(row_count, width))
    near = dot3(all_heads, core_near, NN)
    away = dot3(all_heads, core_away, NN)
    near_pair, away_pair = split(near), split(away)
    score = dot3(near_pair, tail_near, NT) + dot3(away_pair, tail_away, NT)
    chance = 1.0 / (1.0 + jnp.exp(-score))
    for p in z_peers:
        take_z(1, p, count_in.at[:, p])
    rho = uses * chance - count_in[...].reshape(row_count, tail_rows)
    rho_z[w] = rho
    for k in reversed(range(len(z_peers))):
        put_z(2, k, rho_z.at[w], rho_z.at[w])

    for k, p in enumerate(x_peers):
        take_x(0, p, tail_x.at[p, 0])
        put_sub(2 + k, tail_x.at[p, 0], tail_x.at[p, 1])
    kind = 1 + tails

    rho_pair = split(rho)
    weighted = (
        split(dot3(rho_pair, tail_near, NN)),
        split(dot3(rho_pair, tail_away, NN)),
    )
    head_term = dot3(weighted[0], core_near, NT) + dot3(weighted[1], core_away, NT)
    hg[...] = head_term.reshape(tails, wides, part, width)
    for k, p in enumerate(x_peers):
        put_x(1, k, hg.at[p], hg_x.at[t])

    turned = split(rho.T)
    tp_out[...] = dot3(turned, away_pair, NN)
    put_sub(kind, tp_out, tp_in)
    tail_term = dot3(turned, near_pair, NN)

    total = hg[t]
    for p in x_peers:
        take_x(1, p, hg_x.at[p])
        total = total + hg_x[p]
    hg_sum[...] = total
    for k, p in enumerate(z_peers):
        put_z(4, k, hg_sum.at[p], hg_z.at[w])
    take_sub(kind, tp_in)
    tp_sum[...] = (tail_term + tp_in[...]).reshape(wides, tail_rows // wides, half)
    for k, p in enumerate(z_peers):
        put_z(3, k, tp_sum.at[p], tp_z.at[w])

    def take_rho(r):
        @pl.when(r != w)
        def _():
            take_z(2, r, rho_z.at[r])

    for k, p in enumerate(x_peers):
        for i in range(per_tail):
            r = p * per_tail + i
            take_rho(r)
            put_x(2 + i, k, rho_z.at[r], rho_x.at[t, i])
    for i in range(per_tail):
        take_rho(t * per_tail + i)
    for k, p in enumerate(x_peers):
        take_sub(2 + k, tail_x.at[p, 1])
    tail_all = [
        split(jnp.concatenate([own[...]] + [tail_x[p, side] for p in x_peers], axis=0))
        for side, own in enumerate((tail, tail_far))
    ]
    columns = width // wides
    at = pl.multiple_of(w * columns, columns)
    turned_heads = split(heads[:, :, :, pl.ds(at, columns)].reshape(row_count, columns).T)
    kept = []
    for i in range(per_tail):
        for p in x_peers:
            take_x(2 + i, p, rho_x.at[p, i])
        rhos = [rho_z[t * per_tail + i]] + [rho_x[p, i] for p in x_peers]
        rhos = split(jnp.concatenate(rhos, axis=1))
        g_out[i] = dot3(turned_heads, split(dot3(rhos, tail_all[1], NN)), NN)
        put_sub(kind + 1 + i, g_out.at[i], g_in.at[i])
        core_out[i] = dot3(turned_heads, split(dot3(rhos, tail_all[0], NN)), NN)

    total = hg_sum[w]
    for p in z_peers:
        take_z(4, p, hg_z.at[p])
        total = total + hg_z[p]
    head_out[...] = total * scales[0]
    total = tp_sum[w]
    for p in z_peers:
        take_z(3, p, tp_z.at[p])
        total = total + tp_z[p]
    tail_out[0] = total * scales[1]
    for i in range(per_tail):
        take_sub(kind + 1 + i, g_in.at[i])
        core_out[i] = (core_out[i] + g_in[i]) * scales[2]
    for job in sent:
        job.wait_send()


def fused(wides, tails, head_embed, tail_embed, core_mats, labels, core_lists):
    rows, width = head_embed.shape
    tail_rows, half = tail_embed.shape
    slots = core_lists.shape[1]
    part = rows // (2 * tails)
    per_tail = wides // tails
    count = tails * wides * part
    columns = width // wides
    block = tail_rows // wides
    scales = (
        1.0 / math.sqrt(slots * tail_rows * tails),
        1.0 / math.sqrt(slots * rows * wides),
        1.0 / math.sqrt(rows * wides * tail_rows),
    )
    vmem = pl.BlockSpec(memory_space=pltpu.VMEM)
    buffer = lambda *shape: pltpu.VMEM(shape, F32)
    sub_kinds = 1 + tails + 1 + per_tail
    x_kinds = 2 + per_tail
    sems = pltpu.SemaphoreType.DMA
    return pl.pallas_call(
        functools.partial(kernel, wides, tails, per_tail, scales),
        out_shape=(
            jax.ShapeDtypeStruct((part, width), F32),
            jax.ShapeDtypeStruct((1, block, half), F32),
            jax.ShapeDtypeStruct((per_tail, columns, half), F32),
        ),
        in_specs=[pl.BlockSpec(memory_space=pltpu.SMEM)] + [vmem] * 4,
        out_specs=(vmem, vmem, vmem),
        scratch_shapes=[
            buffer(tails, wides, part, width),
            buffer(wides, tails, part, tail_rows),
            buffer(tails, wides, part, tail_rows),
            buffer(width, half),
            buffer(tail_rows, half),
            buffer(tails, 2, tail_rows, half),
            buffer(wides, count, tail_rows),
            buffer(tails, per_tail, count, tail_rows),
            buffer(tail_rows, half),
            buffer(tail_rows, half),
            buffer(wides, block, half),
            buffer(wides, block, half),
            buffer(tails, wides, part, width),
            buffer(tails, wides, part, width),
            buffer(wides, part, width),
            buffer(wides, part, width),
            buffer(per_tail, columns, half),
            buffer(per_tail, columns, half),
            sems((sub_kinds,)),
            sems((sub_kinds,)),
            sems((5, wides)),
            sems((5, wides)),
            sems((x_kinds, tails)),
            sems((x_kinds, tails)),
        ],
        compiler_params=pltpu.CompilerParams(
            collective_id=0, has_side_effects=True, vmem_limit_bytes=40 * 2**20
        ),
    )(core_lists, head_embed, tail_embed, core_mats, labels)


def broadcast(value, axis, source):
    kept = jnp.where(lax.axis_index(axis) == source, value, 0).astype(value.dtype)
    return lax.psum(kept, axis)


def collective(head_embed, tail_embed, core_mats, labels, core_lists):
    highest = lax.Precision.HIGHEST
    slot_count = core_lists.shape[1]
    half_width = tail_embed.shape[1]
    listed = core_lists[0]
    wide_count = lax.axis_size("wide")
    tail_acc = jnp.zeros((tail_embed.shape[0], half_width), jnp.float32)
    head_acc = jnp.zeros(head_embed.shape, jnp.float32)
    core_terms = []
    for slot_index in range(slot_count):
        relation = listed[slot_index]
        owned_count = core_mats.shape[0]
        local_core = lax.dynamic_index_in_dim(core_mats, relation % owned_count, 0, keepdims=False)
        matrix = broadcast(local_core, "wide", relation // owned_count)
        projected = jnp.dot(
            head_embed, matrix, precision=highest, preferred_element_type=jnp.float32
        )
        partial_score = lax.dot_general(
            projected, tail_embed, (((1,), (1,)), ((), ())), precision=highest
        )
        score_tile = lax.psum(partial_score, "sub")
        residual = jax.nn.sigmoid(score_tile) - labels[:, slot_index, :].astype(jnp.float32)
        tail_acc = tail_acc + lax.dot_general(
            residual, projected, (((0,), (0,)), ((), ())), precision=highest
        )
        weighted = jnp.dot(
            residual, tail_embed, precision=highest, preferred_element_type=jnp.float32
        )
        head_acc = head_acc + lax.dot_general(
            weighted, matrix, (((1,), (1,)), ((), ())), precision=highest
        )
        core_term = lax.dot_general(
            head_embed, weighted, (((0,), (0,)), ((), ())), precision=highest
        )
        core_terms.append(core_term)
    core_rows, tail_stack = (
        lax.psum_scatter(jnp.stack(core_terms), "wide", scatter_dimension=1, tiled=True),
        lax.psum_scatter(tail_acc[None], "wide", scatter_dimension=1, tiled=True),
    )
    tail_part = tail_stack[0]
    relation_count = core_mats.shape[0] * wide_count
    selector = (jnp.arange(relation_count, dtype=jnp.int32)[:, None] == listed[None, :]).astype(
        jnp.float32
    )
    combined = jnp.einsum("rj,jab->rab", selector, core_rows, precision=highest)
    heads_total = head_embed.shape[0] * wide_count
    tails_total = tail_embed.shape[0] * lax.axis_size("tail")
    core_grad = lax.psum_scatter(combined, "tail", scatter_dimension=0, tiled=True) * (
        1.0 / math.sqrt(heads_total * tail_embed.shape[0])
    )
    head_grad = lax.psum_scatter(head_acc, ("tail", "sub"), scatter_dimension=0, tiled=True) * (
        1.0 / math.sqrt(slot_count * tails_total)
    )
    tail_grad = (tail_part * (1.0 / math.sqrt(slot_count * heads_total)))[None]
    return (head_grad, tail_grad, core_grad)


def solution(mesh):
    wides, tails, subs = (mesh.shape[name] for name in ("wide", "tail", "sub"))

    def body(head_embed, tail_embed, core_mats, labels, core_lists):
        rows, width = head_embed.shape
        fits = (
            subs == 2
            and core_mats.shape[0] == 1
            and wides % tails == 0
            and rows % (16 * tails) == 0
            and tail_embed.shape[0] % (8 * wides) == 0
            and width % (128 * wides) == 0
        )
        if fits:
            return fused(wides, tails, head_embed, tail_embed, core_mats, labels, core_lists)
        return collective(head_embed, tail_embed, core_mats, labels, core_lists)

    in_specs = (
        P(("groups", "wide"), None),
        P(("groups", "tail"), "sub"),
        P(("groups", "wide"), None, "sub"),
        P(("groups", "wide"), None, "tail"),
        P(("groups", "tail"), None),
    )
    out_specs = (
        P(("groups", "wide", "tail", "sub"), None),
        P(("groups", "tail"), "wide", "sub"),
        P(("groups", "tail"), "wide", "sub"),
    )
    return jax.shard_map(body, mesh=mesh, in_specs=in_specs, out_specs=out_specs, check_vma=False)
```

```python
import functools
import math

import jax
import jax.numpy as jnp
from jax import lax
from jax.experimental import pallas as pl
from jax.experimental.pallas import tpu as pltpu
from jax.sharding import PartitionSpec as P

MESH = pl.DeviceIdType.MESH
F32 = jnp.float32
BF16 = jnp.bfloat16
NN = (((1,), (0,)), ((), ()))
NT = (((1,), (1,)), ((), ()))


def split(value):
    high = value.astype(BF16)
    return high, (value - high.astype(F32)).astype(BF16)


def dot3(a, b, dims):
    one = lambda x, y: lax.dot_general(x, y, dims, preferred_element_type=F32)
    return one(a[0], b[0]) + (one(a[0], b[1]) + one(a[1], b[0]))


def kernel(
    wides, tails, per_tail, scales,
    lists_hbm, head_hbm, tail_hbm, core_hbm, labels_hbm,
    head_out, tail_out, core_out,
    lists, labels, tail, core,
    heads, count_out, count_in, core_far, tail_far, tail_x,
    q_all, q_in, q_sum, q_z, q_x,
    tp_out, tp_in, tp_sum, tp_z, hg, hg_x, hg_sum, hg_z,
    own_sem, sib_send, sib_recv, z_send, z_recv, x_send, x_recv,
):
    w, t, s = lax.axis_index("wide"), lax.axis_index("tail"), lax.axis_index("sub")
    sibling = {"sub": 1 - s}
    z_peers = [lax.rem(w + k, wides) for k in range(1, wides)]
    x_peers = [lax.rem(t + k, tails) for k in range(1, tails)]
    part = heads.shape[2]
    width = heads.shape[3]
    tail_rows, half = tail.shape
    slots = labels.shape[2]
    row_count = tails * wides * part
    columns = width // wides

    def copy(src, dst, send, recv, device):
        return pltpu.make_async_remote_copy(
            src_ref=src, dst_ref=dst, send_sem=send, recv_sem=recv,
            device_id=device, device_id_type=MESH,
        )

    sent = []

    def put(src, dst, send, recv, device):
        job = copy(src, dst, send, recv, device)
        job.start()
        sent.append(job)

    def arrived(dst, send, recv, device):
        copy(dst, dst, send, recv, device).wait_recv()

    def put_sub(kind, src, dst):
        put(src, dst, sib_send.at[kind], sib_recv.at[kind], sibling)

    def take_sub(kind, dst):
        arrived(dst, sib_send.at[kind], sib_recv.at[kind], sibling)

    def put_z(kind, k, src, dst):
        put(src, dst, z_send.at[kind, k], z_recv.at[kind, w], {"wide": z_peers[k]})

    def take_z(kind, p, dst):
        arrived(dst, z_send.at[kind, 0], z_recv.at[kind, p], {"wide": z_peers[0]})

    def put_x(kind, k, src, dst):
        put(src, dst, x_send.at[kind, k], x_recv.at[kind, t], {"tail": x_peers[k]})

    def take_x(kind, p, dst):
        arrived(dst, x_send.at[kind, 0], x_recv.at[kind, p], {"tail": x_peers[0]})

    barrier = pltpu.get_barrier_semaphore()
    partners = [sibling] + [{"wide": p} for p in z_peers] + [{"tail": p} for p in x_peers]
    for device in partners:
        pl.semaphore_signal(barrier, inc=1, device_id=device, device_id_type=MESH)
    own = [
        pltpu.make_async_copy(src, dst, own_sem.at[i])
        for i, (src, dst) in enumerate((
            (lists_hbm, lists),
            (labels_hbm.at[:, s], labels),
            (head_hbm.at[:, s], heads.at[:, w]),
            (core_hbm.at[0], core),
            (tail_hbm, tail),
        ))
    ]
    for job in own:
        job.start()
    pl.semaphore_wait(barrier, len(partners))

    for k in reversed(range(len(z_peers))):
        put_z(0, k, head_hbm.at[:, s], heads.at[:, w])
    put_sub(0, core_hbm.at[0], core_far)
    put_sub(1, tail_hbm, tail_far)
    for k in range(len(x_peers)):
        put_x(0, k, tail_hbm, tail_x.at[t])

    own[0].wait()
    own[1].wait()
    shape = (wides, part, part * slots)
    lane = lax.broadcasted_iota(jnp.int32, shape, 2)
    offset = lane - slots * lax.broadcasted_iota(jnp.int32, shape, 1)
    listed = jnp.full(shape, -1, jnp.int32)
    for j in range(slots):
        listed = jnp.where(offset == j, lists[0, j], listed)
    picks = jnp.where(listed == lax.broadcasted_iota(jnp.int32, shape, 0), 1.0, 0.0)
    picks = picks.reshape(wides * part, part * slots).astype(BF16)
    for tau in range(tails):
        block = labels[tau].reshape(part * slots, tail_rows)
        counts = lax.dot_general(
            picks, block.astype(F32).astype(BF16), NN, preferred_element_type=F32
        )
        count_out[:, tau] = counts.reshape(wides, part, tail_rows)
    for k, p in enumerate(z_peers):
        put_z(1, k, count_out.at[p], count_in.at[:, w])
    count_in[:, w] = count_out[w]
    uses = jnp.float32(0.0)
    for j in range(slots):
        uses = uses + (lists[0, j] == w).astype(F32)

    own[3].wait()
    own[4].wait()
    core_near = split(core[...])
    tail_near = split(tail[...])
    take_sub(0, core_far)
    core_away = split(core_far[...])
    take_sub(1, tail_far)
    tail_away = split(tail_far[...])
    own[2].wait()
    for p in z_peers:
        take_z(0, p, heads.at[:, p])
    head_rows = heads[...].reshape(row_count, width)
    all_heads = split(head_rows)
    near_pair = split(dot3(all_heads, core_near, NN))
    away_pair = split(dot3(all_heads, core_away, NN))
    score = dot3(near_pair, tail_near, NT) + dot3(away_pair, tail_away, NT)
    turned_heads = split(head_rows.T)
    chance = 1.0 / (1.0 + jnp.exp(-score))
    for p in z_peers:
        take_z(1, p, count_in.at[:, p])
    rho = uses * chance - count_in[...].reshape(row_count, tail_rows)
    rho_pair = split(rho)

    q_all[...] = dot3(turned_heads, rho_pair, NN).reshape(wides, 2, columns // 2, tail_rows)
    put_sub(3, q_all.at[:, 1 - s], q_in)

    weighted = (
        split(dot3(rho_pair, tail_near, NN)),
        split(dot3(rho_pair, tail_away, NN)),
    )
    take_sub(3, q_in)
    q_sum[...] = q_all[:, s] + q_in[...]
    for k in reversed(range(len(z_peers))):
        put_z(2, k, q_sum.at[z_peers[k]], q_z.at[w, s])
    q_z[w, s] = q_sum[w]
    head_term = dot3(weighted[0], core_near, NT) + dot3(weighted[1], core_away, NT)
    hg[...] = head_term.reshape(tails, wides, part, width)
    for k, p in enumerate(x_peers):
        put_x(1, k, hg.at[p], hg_x.at[t])

    turned = split(rho.T)
    tp_out[...] = dot3(turned, away_pair, NN)
    put_sub(2, tp_out, tp_in)
    tail_term = dot3(turned, near_pair, NN)

    def take_q(r):
        @pl.when(r != w)
        def _():
            take_z(2, r, q_z.at[r, s])

    for k, p in enumerate(x_peers):
        for i in range(per_tail):
            r = p * per_tail + i
            take_q(r)
            put_x(2 + i, k, q_z.at[r, s], q_x.at[t, i, s])
    for i in range(per_tail):
        r = t * per_tail + i
        take_q(r)
        put_sub(4 + i, q_z.at[r, s], q_z.at[r, s])

    total = hg[t]
    for p in x_peers:
        take_x(1, p, hg_x.at[p])
        total = total + hg_x[p]
    hg_sum[...] = total
    for k, p in enumerate(z_peers):
        put_z(4, k, hg_sum.at[p], hg_z.at[w])
    take_sub(2, tp_in)
    tp_sum[...] = (tail_term + tp_in[...]).reshape(wides, tail_rows // wides, half)
    for k, p in enumerate(z_peers):
        put_z(3, k, tp_sum.at[p], tp_z.at[w])

    for k, p in enumerate(x_peers):
        take_x(0, p, tail_x.at[p])
    tail_all = split(jnp.concatenate([tail[...]] + [tail_x[p] for p in x_peers], axis=0))
    base = 4 + per_tail
    for k, p in enumerate(x_peers):
        for i in range(per_tail):
            take_x(2 + i, p, q_x.at[p, i, s])
            put_sub(base + k * per_tail + i, q_x.at[p, i, s], q_x.at[p, i, s])
    for i in range(per_tail):
        take_sub(4 + i, q_z.at[t * per_tail + i, 1 - s])
    for k, p in enumerate(x_peers):
        for i in range(per_tail):
            take_sub(base + k * per_tail + i, q_x.at[p, i, 1 - s])
    rows = [
        jnp.concatenate(
            [block.reshape(columns, tail_rows) for block in
             [q_z[t * per_tail + i]] + [q_x[p, i] for p in x_peers]],
            axis=1,
        )
        for i in range(per_tail)
    ]
    grads = dot3(split(jnp.concatenate(rows, axis=0)), tail_all, NN)
    core_out[...] = grads.reshape(per_tail, columns, half) * scales[2]

    total = hg_sum[w]
    for p in z_peers:
        take_z(4, p, hg_z.at[p])
        total = total + hg_z[p]
    head_out[...] = total * scales[0]
    total = tp_sum[w]
    for p in z_peers:
        take_z(3, p, tp_z.at[p])
        total = total + tp_z[p]
    tail_out[0] = total * scales[1]
    for job in sent:
        job.wait_send()


def store(count, *refs):
    sources, targets, sems = refs[:count], refs[count:2 * count], refs[2 * count]
    jobs = [
        pltpu.make_async_copy(source, target, sems.at[i])
        for i, (source, target) in enumerate(zip(sources, targets))
    ]
    for job in jobs:
        job.start()
    for job in jobs:
        job.wait()


def fused(wides, tails, head_embed, tail_embed, core_mats, labels, core_lists):
    rows, width = head_embed.shape
    tail_rows, half = tail_embed.shape
    slots = core_lists.shape[1]
    part = rows // (2 * tails)
    per_tail = wides // tails
    columns = width // wides
    block = tail_rows // wides
    scales = (
        1.0 / math.sqrt(slots * tail_rows * tails),
        1.0 / math.sqrt(slots * rows * wides),
        1.0 / math.sqrt(rows * wides * tail_rows),
    )
    hbm = pl.BlockSpec(memory_space=pltpu.HBM)
    vmem = pl.BlockSpec(memory_space=pltpu.VMEM)
    buffer = lambda *shape: pltpu.VMEM(shape, F32)
    sub_kinds = 4 + per_tail * tails
    x_kinds = 2 + per_tail
    sems = pltpu.SemaphoreType.DMA
    shapes = (
        jax.ShapeDtypeStruct((part, width), F32),
        jax.ShapeDtypeStruct((1, block, half), F32),
        jax.ShapeDtypeStruct((per_tail, columns, half), F32),
    )
    results = pl.pallas_call(
        functools.partial(kernel, wides, tails, per_tail, scales),
        out_shape=shapes,
        in_specs=[hbm] * 5,
        out_specs=(vmem,) * 3,
        scratch_shapes=[
            pltpu.SMEM((1, slots), jnp.int32),
            pltpu.VMEM((tails, part, slots, tail_rows), jnp.int32),
            buffer(tail_rows, half),
            buffer(width, half),
            buffer(tails, wides, part, width),
            buffer(wides, tails, part, tail_rows),
            buffer(tails, wides, part, tail_rows),
            buffer(width, half),
            buffer(tail_rows, half),
            buffer(tails, tail_rows, half),
            buffer(wides, 2, columns // 2, tail_rows),
            buffer(wides, columns // 2, tail_rows),
            buffer(wides, columns // 2, tail_rows),
            buffer(wides, 2, columns // 2, tail_rows),
            buffer(tails, per_tail, 2, columns // 2, tail_rows),
            buffer(tail_rows, half),
            buffer(tail_rows, half),
            buffer(wides, block, half),
            buffer(wides, block, half),
            buffer(tails, wides, part, width),
            buffer(tails, wides, part, width),
            buffer(wides, part, width),
            buffer(wides, part, width),
            sems((5,)),
            sems((sub_kinds,)),
            sems((sub_kinds,)),
            sems((5, wides)),
            sems((5, wides)),
            sems((x_kinds, tails)),
            sems((x_kinds, tails)),
        ],
        compiler_params=pltpu.CompilerParams(
            collective_id=0, has_side_effects=True, vmem_limit_bytes=40 * 2**20
        ),
    )(*[
        pltpu.with_memory_space_constraint(value, pltpu.HBM)
        for value in (
            core_lists,
            head_embed.reshape(tails, 2, part, width),
            tail_embed,
            core_mats,
            labels.reshape(tails, 2, part, slots, tail_rows),
        )
    ])
    return pl.pallas_call(
        functools.partial(store, len(shapes)),
        out_shape=shapes,
        in_specs=[vmem] * 3,
        out_specs=(hbm,) * 3,
        scratch_shapes=[sems((3,))],
    )(*[pltpu.with_memory_space_constraint(value, pltpu.VMEM) for value in results])


def broadcast(value, axis, source):
    kept = jnp.where(lax.axis_index(axis) == source, value, 0).astype(value.dtype)
    return lax.psum(kept, axis)


def collective(head_embed, tail_embed, core_mats, labels, core_lists):
    highest = lax.Precision.HIGHEST
    slot_count = core_lists.shape[1]
    half_width = tail_embed.shape[1]
    listed = core_lists[0]
    wide_count = lax.axis_size("wide")
    tail_acc = jnp.zeros((tail_embed.shape[0], half_width), jnp.float32)
    head_acc = jnp.zeros(head_embed.shape, jnp.float32)
    core_terms = []
    for slot_index in range(slot_count):
        relation = listed[slot_index]
        owned_count = core_mats.shape[0]
        local_core = lax.dynamic_index_in_dim(core_mats, relation % owned_count, 0, keepdims=False)
        matrix = broadcast(local_core, "wide", relation // owned_count)
        projected = jnp.dot(
            head_embed, matrix, precision=highest, preferred_element_type=jnp.float32
        )
        partial_score = lax.dot_general(
            projected, tail_embed, (((1,), (1,)), ((), ())), precision=highest
        )
        score_tile = lax.psum(partial_score, "sub")
        residual = jax.nn.sigmoid(score_tile) - labels[:, slot_index, :].astype(jnp.float32)
        tail_acc = tail_acc + lax.dot_general(
            residual, projected, (((0,), (0,)), ((), ())), precision=highest
        )
        weighted = jnp.dot(
            residual, tail_embed, precision=highest, preferred_element_type=jnp.float32
        )
        head_acc = head_acc + lax.dot_general(
            weighted, matrix, (((1,), (1,)), ((), ())), precision=highest
        )
        core_term = lax.dot_general(
            head_embed, weighted, (((0,), (0,)), ((), ())), precision=highest
        )
        core_terms.append(core_term)
    core_rows, tail_stack = (
        lax.psum_scatter(jnp.stack(core_terms), "wide", scatter_dimension=1, tiled=True),
        lax.psum_scatter(tail_acc[None], "wide", scatter_dimension=1, tiled=True),
    )
    tail_part = tail_stack[0]
    relation_count = core_mats.shape[0] * wide_count
    selector = (jnp.arange(relation_count, dtype=jnp.int32)[:, None] == listed[None, :]).astype(
        jnp.float32
    )
    combined = jnp.einsum("rj,jab->rab", selector, core_rows, precision=highest)
    heads_total = head_embed.shape[0] * wide_count
    tails_total = tail_embed.shape[0] * lax.axis_size("tail")
    core_grad = lax.psum_scatter(combined, "tail", scatter_dimension=0, tiled=True) * (
        1.0 / math.sqrt(heads_total * tail_embed.shape[0])
    )
    head_grad = lax.psum_scatter(head_acc, ("tail", "sub"), scatter_dimension=0, tiled=True) * (
        1.0 / math.sqrt(slot_count * tails_total)
    )
    tail_grad = (tail_part * (1.0 / math.sqrt(slot_count * heads_total)))[None]
    return (head_grad, tail_grad, core_grad)


def solution(mesh):
    wides, tails, subs = (mesh.shape[name] for name in ("wide", "tail", "sub"))

    def body(head_embed, tail_embed, core_mats, labels, core_lists):
        rows, width = head_embed.shape
        fits = (
            subs == 2
            and core_mats.shape[0] == 1
            and wides % tails == 0
            and rows % (16 * tails) == 0
            and tail_embed.shape[0] % (8 * wides) == 0
            and width % (128 * wides) == 0
        )
        if fits:
            return fused(wides, tails, head_embed, tail_embed, core_mats, labels, core_lists)
        return collective(head_embed, tail_embed, core_mats, labels, core_lists)

    in_specs = (
        P(("groups", "wide"), None),
        P(("groups", "tail"), "sub"),
        P(("groups", "wide"), None, "sub"),
        P(("groups", "wide"), None, "tail"),
        P(("groups", "tail"), None),
    )
    out_specs = (
        P(("groups", "wide", "tail", "sub"), None),
        P(("groups", "tail"), "wide", "sub"),
        P(("groups", "tail"), "wide", "sub"),
    )
    return jax.shard_map(body, mesh=mesh, in_specs=in_specs, out_specs=out_specs, check_vma=False)
```

```python
import functools
import math

import jax
import jax.numpy as jnp
from jax import lax
from jax.experimental import pallas as pl
from jax.experimental.pallas import tpu as pltpu
from jax.sharding import PartitionSpec as P

MESH = pl.DeviceIdType.MESH
F32 = jnp.float32
BF16 = jnp.bfloat16
NN = (((1,), (0,)), ((), ()))
NT = (((1,), (1,)), ((), ()))


def split(value):
    high = value.astype(BF16)
    return high, (value - high.astype(F32)).astype(BF16)


def dot3(a, b, dims):
    one = lambda x, y: lax.dot_general(x, y, dims, preferred_element_type=F32)
    return one(a[0], b[0]) + (one(a[0], b[1]) + one(a[1], b[0]))


def kernel(
    wides, tails, per_tail, scales,
    lists_hbm, head_hbm, tail_hbm, core_hbm, labels_hbm,
    head_out, tail_out, core_out,
    lists, labels, tail, core,
    heads, count_out, count_in, core_far, tail_far, tail_x,
    q_all, q_in, q_sum, q_z, q_x,
    tp_out, tp_in, tp_sum, tp_z, hg, hg_x, hg_sum, hg_z,
    own_sem, sib_send, sib_recv, z_send, z_recv, x_send, x_recv,
):
    w, t, s = lax.axis_index("wide"), lax.axis_index("tail"), lax.axis_index("sub")
    sibling = {"sub": 1 - s}
    z_peers = [lax.rem(w + k, wides) for k in range(1, wides)]
    x_peers = [lax.rem(t + k, tails) for k in range(1, tails)]
    part = heads.shape[2]
    width = heads.shape[3]
    tail_rows, half = tail.shape
    slots = labels.shape[2]
    row_count = tails * wides * part
    columns = width // wides

    def copy(src, dst, send, recv, device):
        return pltpu.make_async_remote_copy(
            src_ref=src, dst_ref=dst, send_sem=send, recv_sem=recv,
            device_id=device, device_id_type=MESH,
        )

    sent = []

    def put(src, dst, send, recv, device):
        job = copy(src, dst, send, recv, device)
        job.start()
        sent.append(job)

    def arrived(dst, send, recv, device):
        copy(dst, dst, send, recv, device).wait_recv()

    def put_sub(kind, src, dst):
        put(src, dst, sib_send.at[kind], sib_recv.at[kind], sibling)

    def take_sub(kind, dst):
        arrived(dst, sib_send.at[kind], sib_recv.at[kind], sibling)

    def put_z(kind, k, src, dst):
        put(src, dst, z_send.at[kind, k], z_recv.at[kind, w], {"wide": z_peers[k]})

    def take_z(kind, p, dst):
        arrived(dst, z_send.at[kind, 0], z_recv.at[kind, p], {"wide": z_peers[0]})

    def put_x(kind, k, src, dst):
        put(src, dst, x_send.at[kind, k], x_recv.at[kind, t], {"tail": x_peers[k]})

    def take_x(kind, p, dst):
        arrived(dst, x_send.at[kind, 0], x_recv.at[kind, p], {"tail": x_peers[0]})

    barrier = pltpu.get_barrier_semaphore()
    partners = [sibling] + [{"wide": p} for p in z_peers] + [{"tail": p} for p in x_peers]
    for device in partners:
        pl.semaphore_signal(barrier, inc=1, device_id=device, device_id_type=MESH)
    own = [
        pltpu.make_async_copy(src, dst, own_sem.at[i])
        for i, (src, dst) in enumerate((
            (lists_hbm, lists),
            (labels_hbm.at[:, s], labels),
            (head_hbm.at[:, s], heads.at[:, w]),
            (core_hbm.at[0], core),
            (tail_hbm, tail),
        ))
    ]
    for job in own:
        job.start()
    pl.semaphore_wait(barrier, len(partners))

    for k in reversed(range(len(z_peers))):
        put_z(0, k, head_hbm.at[:, s], heads.at[:, w])
    put_sub(0, core_hbm.at[0], core_far)
    put_sub(1, tail_hbm, tail_far)
    for k in range(len(x_peers)):
        put_x(0, k, tail_hbm, tail_x.at[t])

    own[0].wait()
    own[1].wait()
    shape = (wides, part, part * slots)
    lane = lax.broadcasted_iota(jnp.int32, shape, 2)
    offset = lane - slots * lax.broadcasted_iota(jnp.int32, shape, 1)
    listed = jnp.full(shape, -1, jnp.int32)
    for j in range(slots):
        listed = jnp.where(offset == j, lists[0, j], listed)
    picks = jnp.where(listed == lax.broadcasted_iota(jnp.int32, shape, 0), 1.0, 0.0)
    picks = picks.reshape(wides * part, part * slots).astype(BF16)
    for tau in range(tails):
        block = labels[tau].reshape(part * slots, tail_rows)
        counts = lax.dot_general(
            picks, block.astype(F32).astype(BF16), NN, preferred_element_type=F32
        )
        count_out[:, tau] = counts.reshape(wides, part, tail_rows)
    for k, p in enumerate(z_peers):
        put_z(1, k, count_out.at[p], count_in.at[:, w])
    count_in[:, w] = count_out[w]
    uses = jnp.float32(0.0)
    for j in range(slots):
        uses = uses + (lists[0, j] == w).astype(F32)

    own[3].wait()
    own[4].wait()
    core_near = split(core[...])
    tail_near = split(tail[...])
    take_sub(0, core_far)
    core_away = split(core_far[...])
    take_sub(1, tail_far)
    tail_away = split(tail_far[...])
    own[2].wait()
    for p in z_peers:
        take_z(0, p, heads.at[:, p])
    head_rows = heads[...].reshape(row_count, width)
    all_heads = split(head_rows)
    near_pair = split(dot3(all_heads, core_near, NN))
    away_pair = split(dot3(all_heads, core_away, NN))
    score = dot3(near_pair, tail_near, NT) + dot3(away_pair, tail_away, NT)
    turned_heads = split(head_rows.T)
    chance = 1.0 / (1.0 + jnp.exp(-score))
    for p in z_peers:
        take_z(1, p, count_in.at[:, p])
    rho = uses * chance - count_in[...].reshape(row_count, tail_rows)
    rho_pair = split(rho)

    q_all[...] = dot3(turned_heads, rho_pair, NN).reshape(wides, 2, columns // 2, tail_rows)
    put_sub(3, q_all.at[:, 1 - s], q_in)

    turned = split(rho.T)
    tp_out[...] = dot3(turned, away_pair, NN)
    put_sub(2, tp_out, tp_in)

    weighted = (
        split(dot3(rho_pair, tail_near, NN)),
        split(dot3(rho_pair, tail_away, NN)),
    )
    take_sub(3, q_in)
    q_sum[...] = q_all[:, s] + q_in[...]
    for k in reversed(range(len(z_peers))):
        put_z(2, k, q_sum.at[z_peers[k]], q_z.at[w, s])
    q_z[w, s] = q_sum[w]
    head_term = dot3(weighted[0], core_near, NT) + dot3(weighted[1], core_away, NT)
    hg[...] = head_term.reshape(tails, wides, part, width)
    for k, p in enumerate(x_peers):
        put_x(1, k, hg.at[p], hg_x.at[t])

    tail_term = dot3(turned, near_pair, NN)
    take_sub(2, tp_in)
    tp_sum[...] = (tail_term + tp_in[...]).reshape(wides, tail_rows // wides, half)
    for k, p in enumerate(z_peers):
        put_z(3, k, tp_sum.at[p], tp_z.at[w])

    total = hg[t]
    for p in x_peers:
        take_x(1, p, hg_x.at[p])
        total = total + hg_x[p]
    hg_sum[...] = total
    for k, p in enumerate(z_peers):
        put_z(4, k, hg_sum.at[p], hg_z.at[w])
    def take_q(r):
        @pl.when(r != w)
        def _():
            take_z(2, r, q_z.at[r, s])

    for k, p in enumerate(x_peers):
        for i in range(per_tail):
            r = p * per_tail + i
            take_q(r)
            put_x(2 + i, k, q_z.at[r, s], q_x.at[t, i, s])
    for i in range(per_tail):
        r = t * per_tail + i
        take_q(r)
        put_sub(4 + i, q_z.at[r, s], q_z.at[r, s])

    for k, p in enumerate(x_peers):
        take_x(0, p, tail_x.at[p])
    tail_all = split(jnp.concatenate([tail[...]] + [tail_x[p] for p in x_peers], axis=0))
    base = 4 + per_tail
    for k, p in enumerate(x_peers):
        for i in range(per_tail):
            take_x(2 + i, p, q_x.at[p, i, s])
            put_sub(base + k * per_tail + i, q_x.at[p, i, s], q_x.at[p, i, s])
    for i in range(per_tail):
        take_sub(4 + i, q_z.at[t * per_tail + i, 1 - s])
    for k, p in enumerate(x_peers):
        for i in range(per_tail):
            take_sub(base + k * per_tail + i, q_x.at[p, i, 1 - s])
    rows = [
        jnp.concatenate(
            [block.reshape(columns, tail_rows) for block in
             [q_z[t * per_tail + i]] + [q_x[p, i] for p in x_peers]],
            axis=1,
        )
        for i in range(per_tail)
    ]
    grads = dot3(split(jnp.concatenate(rows, axis=0)), tail_all, NN)
    core_out[...] = grads.reshape(per_tail, columns, half) * scales[2]

    total = hg_sum[w]
    for p in z_peers:
        take_z(4, p, hg_z.at[p])
        total = total + hg_z[p]
    head_out[...] = total * scales[0]
    total = tp_sum[w]
    for p in z_peers:
        take_z(3, p, tp_z.at[p])
        total = total + tp_z[p]
    tail_out[0] = total * scales[1]
    for job in sent:
        job.wait_send()


def store(count, *refs):
    sources, targets, sems = refs[:count], refs[count:2 * count], refs[2 * count]
    jobs = [
        pltpu.make_async_copy(source, target, sems.at[i])
        for i, (source, target) in enumerate(zip(sources, targets))
    ]
    for job in jobs:
        job.start()
    for job in jobs:
        job.wait()


def fused(wides, tails, head_embed, tail_embed, core_mats, labels, core_lists):
    rows, width = head_embed.shape
    tail_rows, half = tail_embed.shape
    slots = core_lists.shape[1]
    part = rows // (2 * tails)
    per_tail = wides // tails
    columns = width // wides
    block = tail_rows // wides
    scales = (
        1.0 / math.sqrt(slots * tail_rows * tails),
        1.0 / math.sqrt(slots * rows * wides),
        1.0 / math.sqrt(rows * wides * tail_rows),
    )
    hbm = pl.BlockSpec(memory_space=pltpu.HBM)
    vmem = pl.BlockSpec(memory_space=pltpu.VMEM)
    buffer = lambda *shape: pltpu.VMEM(shape, F32)
    sub_kinds = 4 + per_tail * tails
    x_kinds = 2 + per_tail
    sems = pltpu.SemaphoreType.DMA
    shapes = (
        jax.ShapeDtypeStruct((part, width), F32),
        jax.ShapeDtypeStruct((1, block, half), F32),
        jax.ShapeDtypeStruct((per_tail, columns, half), F32),
    )
    results = pl.pallas_call(
        functools.partial(kernel, wides, tails, per_tail, scales),
        out_shape=shapes,
        in_specs=[hbm] * 5,
        out_specs=(vmem,) * 3,
        scratch_shapes=[
            pltpu.SMEM((1, slots), jnp.int32),
            pltpu.VMEM((tails, part, slots, tail_rows), jnp.int32),
            buffer(tail_rows, half),
            buffer(width, half),
            buffer(tails, wides, part, width),
            buffer(wides, tails, part, tail_rows),
            buffer(tails, wides, part, tail_rows),
            buffer(width, half),
            buffer(tail_rows, half),
            buffer(tails, tail_rows, half),
            buffer(wides, 2, columns // 2, tail_rows),
            buffer(wides, columns // 2, tail_rows),
            buffer(wides, columns // 2, tail_rows),
            buffer(wides, 2, columns // 2, tail_rows),
            buffer(tails, per_tail, 2, columns // 2, tail_rows),
            buffer(tail_rows, half),
            buffer(tail_rows, half),
            buffer(wides, block, half),
            buffer(wides, block, half),
            buffer(tails, wides, part, width),
            buffer(tails, wides, part, width),
            buffer(wides, part, width),
            buffer(wides, part, width),
            sems((5,)),
            sems((sub_kinds,)),
            sems((sub_kinds,)),
            sems((5, wides)),
            sems((5, wides)),
            sems((x_kinds, tails)),
            sems((x_kinds, tails)),
        ],
        compiler_params=pltpu.CompilerParams(
            collective_id=0, has_side_effects=True, vmem_limit_bytes=40 * 2**20
        ),
    )(*[
        pltpu.with_memory_space_constraint(value, pltpu.HBM)
        for value in (
            core_lists,
            head_embed.reshape(tails, 2, part, width),
            tail_embed,
            core_mats,
            labels.reshape(tails, 2, part, slots, tail_rows),
        )
    ])
    return pl.pallas_call(
        functools.partial(store, len(shapes)),
        out_shape=shapes,
        in_specs=[vmem] * 3,
        out_specs=(hbm,) * 3,
        scratch_shapes=[sems((3,))],
    )(*[pltpu.with_memory_space_constraint(value, pltpu.VMEM) for value in results])


def broadcast(value, axis, source):
    kept = jnp.where(lax.axis_index(axis) == source, value, 0).astype(value.dtype)
    return lax.psum(kept, axis)


def collective(head_embed, tail_embed, core_mats, labels, core_lists):
    highest = lax.Precision.HIGHEST
    slot_count = core_lists.shape[1]
    half_width = tail_embed.shape[1]
    listed = core_lists[0]
    wide_count = lax.axis_size("wide")
    tail_acc = jnp.zeros((tail_embed.shape[0], half_width), jnp.float32)
    head_acc = jnp.zeros(head_embed.shape, jnp.float32)
    core_terms = []
    for slot_index in range(slot_count):
        relation = listed[slot_index]
        owned_count = core_mats.shape[0]
        local_core = lax.dynamic_index_in_dim(core_mats, relation % owned_count, 0, keepdims=False)
        matrix = broadcast(local_core, "wide", relation // owned_count)
        projected = jnp.dot(
            head_embed, matrix, precision=highest, preferred_element_type=jnp.float32
        )
        partial_score = lax.dot_general(
            projected, tail_embed, (((1,), (1,)), ((), ())), precision=highest
        )
        score_tile = lax.psum(partial_score, "sub")
        residual = jax.nn.sigmoid(score_tile) - labels[:, slot_index, :].astype(jnp.float32)
        tail_acc = tail_acc + lax.dot_general(
            residual, projected, (((0,), (0,)), ((), ())), precision=highest
        )
        weighted = jnp.dot(
            residual, tail_embed, precision=highest, preferred_element_type=jnp.float32
        )
        head_acc = head_acc + lax.dot_general(
            weighted, matrix, (((1,), (1,)), ((), ())), precision=highest
        )
        core_term = lax.dot_general(
            head_embed, weighted, (((0,), (0,)), ((), ())), precision=highest
        )
        core_terms.append(core_term)
    core_rows, tail_stack = (
        lax.psum_scatter(jnp.stack(core_terms), "wide", scatter_dimension=1, tiled=True),
        lax.psum_scatter(tail_acc[None], "wide", scatter_dimension=1, tiled=True),
    )
    tail_part = tail_stack[0]
    relation_count = core_mats.shape[0] * wide_count
    selector = (jnp.arange(relation_count, dtype=jnp.int32)[:, None] == listed[None, :]).astype(
        jnp.float32
    )
    combined = jnp.einsum("rj,jab->rab", selector, core_rows, precision=highest)
    heads_total = head_embed.shape[0] * wide_count
    tails_total = tail_embed.shape[0] * lax.axis_size("tail")
    core_grad = lax.psum_scatter(combined, "tail", scatter_dimension=0, tiled=True) * (
        1.0 / math.sqrt(heads_total * tail_embed.shape[0])
    )
    head_grad = lax.psum_scatter(head_acc, ("tail", "sub"), scatter_dimension=0, tiled=True) * (
        1.0 / math.sqrt(slot_count * tails_total)
    )
    tail_grad = (tail_part * (1.0 / math.sqrt(slot_count * heads_total)))[None]
    return (head_grad, tail_grad, core_grad)


def solution(mesh):
    wides, tails, subs = (mesh.shape[name] for name in ("wide", "tail", "sub"))

    def body(head_embed, tail_embed, core_mats, labels, core_lists):
        rows, width = head_embed.shape
        fits = (
            subs == 2
            and core_mats.shape[0] == 1
            and wides % tails == 0
            and rows % (16 * tails) == 0
            and tail_embed.shape[0] % (8 * wides) == 0
            and width % (128 * wides) == 0
        )
        if fits:
            return fused(wides, tails, head_embed, tail_embed, core_mats, labels, core_lists)
        return collective(head_embed, tail_embed, core_mats, labels, core_lists)

    in_specs = (
        P(("groups", "wide"), None),
        P(("groups", "tail"), "sub"),
        P(("groups", "wide"), None, "sub"),
        P(("groups", "wide"), None, "tail"),
        P(("groups", "tail"), None),
    )
    out_specs = (
        P(("groups", "wide", "tail", "sub"), None),
        P(("groups", "tail"), "wide", "sub"),
        P(("groups", "tail"), "wide", "sub"),
    )
    return jax.shard_map(body, mesh=mesh, in_specs=in_specs, out_specs=out_specs, check_vma=False)
```
